32 devices in a mesh: groups: 2 (over y), seq: 4 (over z), head: 4 (over x, core).
Axes of the slice: x: 2, y: 2, z: 4, core: 2. Of those that a mesh axis runs over, the one named last changes fastest.
Arguments:
- hit_features: bfloat16 [256, 12288], P('head', ('groups', 'seq')), parts along dimension 1, may hold values from -6 to 6
- depth_kernel: bfloat16 [7, 256], P(None, 'head'), may hold values from -2 to 2
- point_weight: bfloat16 [800, 256], P('head'), may hold values from -0.375 to 0.375
- pair_weight: float32 [8, 3], P('head'), may hold values from -45 to 45
- hit_order: int32 [12288], P(('groups', 'seq')), parts along dimension 0, may hold values from 0 to 1535, as said below
- valid_counts: int32 [8], P(('groups', 'seq')), parts along dimension 0, may hold values from 768 to 1536, as said below
Outputs:
- attended: bfloat16 [256, 12288], P('head', ('groups', 'seq')), parts along dimension 1
The draws below stay inside these ranges and needn't reach their ends.
There are 2 independent parts, one for each index of `groups`. The reference program is written for one: setup_inputs(seed, part) draws one part's arguments, and reference() takes and returns one part's arrays. A program takes and returns all parts, laid end to end along the dimension named above; an argument that names none is the same for every part. Nothing has to cross between parts.
Inputs may be any that keep to these rules, and one draw needn't show every extreme that they name: `hit_order`: each aligned block of 1536 entries is a permutation of 0 .. 1535. `valid_counts`: in every draw one block is full and one holds exactly 768 real hits.
All inputs are finite; a program needn't handle non-finite values.
Results may differ from the reference program's by a relative error of at most 0.0045.
The reference program's roundings to bfloat16 on the way count: a program that leaves them out, or rounds other values in their place, can miss the bound.
Values may be sent and summed in bfloat16 or wider, within the bound.
A program may use at most 64 MiB of HBM per device.

```python
import jax
import jax.numpy as jnp
from jax import lax

C = 256
HEADS = 8
HD = 32
KSIZE = 7
PROJ = 100
HIT_DEV = 1536
HITS = 6144
NBLOCKS = 4


def draw_pair_weight(key, part):
    base_draw = jax.random.uniform(jax.random.fold_in(key, 11), (HEADS, 3), jnp.float32, -1.5, 1.5)
    return base_draw


def draw_hit_order(key, part):
    block_keys = jax.random.split(jax.random.fold_in(key, 21), NBLOCKS)
    orders = jax.vmap(lambda single: jax.random.permutation(single, HIT_DEV))(block_keys)
    return orders.reshape(-1).astype(jnp.int32)


def draw_valid_counts(key, part):
    counts_drawn = jax.random.randint(jax.random.fold_in(key, 31), (NBLOCKS,), HIT_DEV // 2, HIT_DEV + 1)
    shuffled = jax.random.permutation(jax.random.fold_in(key, 32), NBLOCKS)
    counts_drawn = counts_drawn.at[shuffled[0]].set(HIT_DEV).at[shuffled[1]].set(HIT_DEV // 2)
    return counts_drawn.astype(jnp.int32)


def shard_levels(own_key, dims, cuts, low, largest):
    factor_of, own = 1.0, jax.random.fold_in(own_key, 6)
    for dim, shards_of in cuts:
        draws = jnp.exp(jax.random.uniform(jax.random.fold_in(own, dim), (shards_of,), jnp.float32, low / len(cuts), largest / len(cuts)))
        factor_of = factor_of * jnp.repeat(draws, dims[dim] // shards_of).reshape([-1 if axis == dim else 1 for axis in range(len(dims))])
    return factor_of


def centred(key, dims, width, reach, cuts=(), held_as=jnp.bfloat16):
    gain = shard_levels(key, dims, cuts, -0.22, 0.18) if cuts else 1.0
    entries = jax.random.normal(key, dims, jnp.float32) * width * gain
    return jnp.minimum(jnp.maximum(entries, -reach), reach).astype(held_as)


def setup_inputs(seed: int = 0, part: int = 0) -> dict:
    streams_of = jax.random.split(jax.random.key(seed), 7)
    own_keys = jax.random.split(jax.random.fold_in(streams_of[6], part), 7)
    return {
        "hit_features": centred(own_keys[0], (C, HITS), 1.0, 6.0, ((0, 4), (1, 4))),
        "depth_kernel": centred(streams_of[1], (KSIZE, C), KSIZE ** -0.5, 2.0, ((1, 4),)),
        "point_weight": centred(streams_of[2], (HEADS * PROJ, C), C ** -0.5, 0.375, ((0, 4),)),
        "pair_weight": draw_pair_weight(jax.random.fold_in(streams_of[6], 71), part),
        "hit_order": draw_hit_order(jax.random.fold_in(jax.random.fold_in(streams_of[6], part), 71), part),
        "valid_counts": draw_valid_counts(jax.random.fold_in(jax.random.fold_in(streams_of[6], part), 71), part),
    }


floor_pt = 0.1
mass_offset = 0.1
masked_score = -1e+30

def kinematics(raw_vector):
    hit_mass = mass_offset + jax.nn.softplus(raw_vector[0])
    along_x = raw_vector[1]
    along_y = raw_vector[2]
    along_z = raw_vector[3]
    mass_sq = hit_mass * hit_mass
    trans_sq = along_x * along_x + along_y * along_y
    energy = jnp.sqrt(mass_sq + trans_sq + along_z * along_z)
    trans_mass = jnp.sqrt(mass_sq + trans_sq)
    magnitude = jnp.log((jnp.abs(along_z) + energy) / trans_mass)
    rapidity = jnp.where(along_z < 0.0, -magnitude, magnitude)
    inverse_pt = 1.0 / jnp.maximum(jnp.sqrt(trans_sq), floor_pt)
    return jnp.stack([energy, along_x, along_y, along_z, mass_sq, rapidity, along_x * inverse_pt, along_y * inverse_pt, trans_sq])

def pair_bias(query_side, key_side, weights_row):
    left = query_side[:, :, None]
    right = key_side[:, None, :]
    minkowski = left[0] * right[0] - left[1] * right[1] - left[2] * right[2] - left[3] * right[3]
    invariant = left[4] + right[4] + 2.0 * minkowski
    separation = (left[5] - right[5]) ** 2 + 2.0 * (1.0 - left[6] * right[6] - left[7] * right[7])
    kt_sq = jnp.minimum(left[8], right[8]) * separation
    return weights_row[0] * jnp.log(invariant) + weights_row[1] * jnp.log1p(kt_sq) + weights_row[2] * jnp.log1p(separation)

def one_head(args):
    queries, query_kin, keys, values, key_kin, weights_row, key_valid = args
    scores = jnp.dot(queries.T, keys, preferred_element_type=jnp.float32) * HD ** (-0.5)
    scores = scores + pair_bias(query_kin, key_kin, weights_row)
    scores = jnp.where(key_valid[None, :], scores, masked_score)
    row_max = lax.optimization_barrier(jnp.max(scores, axis=1, keepdims=True))
    weights_full = jnp.exp(scores - row_max)
    total = lax.optimization_barrier(jnp.sum(weights_full, axis=1))
    weights_low = weights_full.astype(jnp.bfloat16)
    summed = jnp.dot(values, weights_low.T, preferred_element_type=jnp.float32)
    return (summed / total[None, :]).astype(jnp.bfloat16)

def wrap_ends(array):
    return jnp.concatenate([array[..., -HIT_DEV:], array, array[..., :2 * HIT_DEV]], axis=-1)

def reference(hit_features, depth_kernel, point_weight, pair_weight, hit_order, valid_counts):
    hits = hit_features.shape[1]
    blocks = hits // HIT_DEV
    position = jnp.arange(hits, dtype=jnp.int32)
    block_of = position // HIT_DEV
    ordered = jnp.take(hit_features, (block_of * HIT_DEV + hit_order).astype(jnp.int32), axis=1)
    half = KSIZE // 2
    padded = jnp.pad(ordered, ((0, 0), (half, half))).astype(jnp.float32)
    taps = depth_kernel.astype(jnp.float32)
    summed = jnp.zeros((ordered.shape[0], hits), jnp.float32)
    for offset in range(KSIZE):
        summed = summed + taps[offset][:, None] * padded[:, offset:offset + hits]
    smoothed = summed.astype(jnp.bfloat16)
    projected = jnp.dot(point_weight, smoothed, preferred_element_type=jnp.float32)
    stored = projected.reshape(HEADS, PROJ, hits).astype(jnp.bfloat16)
    queries = stored[:, :HD]
    keys = stored[:, HD:2 * HD]
    values = stored[:, 2 * HD:3 * HD]
    kinetic = jax.vmap(kinematics)(stored[:, 3 * HD:].astype(jnp.float32))
    valid = position % HIT_DEV < valid_counts[block_of]
    keys_padded = wrap_ends(keys)
    values_padded = wrap_ends(values)
    kin_padded = wrap_ends(kinetic)
    valid_padded = wrap_ends(valid)

    def one_block(block_index):
        start = (block_index * HIT_DEV).astype(jnp.int32)
        query_rows = lax.dynamic_slice_in_dim(queries, start, HIT_DEV, 2)
        query_kin = lax.dynamic_slice_in_dim(kinetic, start, HIT_DEV, 2)
        key_rows = lax.dynamic_slice_in_dim(keys_padded, start, 4 * HIT_DEV, 2)
        value_rows = lax.dynamic_slice_in_dim(values_padded, start, 4 * HIT_DEV, 2)
        key_kin = lax.dynamic_slice_in_dim(kin_padded, start, 4 * HIT_DEV, 2)
        key_valid = lax.dynamic_slice_in_dim(valid_padded, start, 4 * HIT_DEV, 0)
        key_valid_all = jnp.broadcast_to(key_valid, (HEADS, 4 * HIT_DEV))
        return lax.map(one_head, (query_rows, query_kin, key_rows, value_rows, key_kin, pair_weight, key_valid_all))
    outputs = lax.map(one_block, jnp.arange(blocks, dtype=jnp.int32))
    return outputs.transpose(1, 2, 0, 3).reshape(HEADS * HD, hits)
```

```python
import functools

import jax
import jax.numpy as jnp
from jax import lax
from jax.experimental import pallas as pl
from jax.experimental.pallas import tpu as pltpu
from jax.sharding import PartitionSpec as P

HD = 32
KSIZE = 7
PROJ = 100

floor_pt = 0.1
mass_offset = 0.1
masked_score = -1e30
LOG2E = 1.4426950408889634

DEPTH = 128
ROW_MASK = 64
ROW_M = 65
ROW_D = 80
ROW_TS = 105

PAIRS = ((0, 0), (0, 1), (1, 0), (1, 1), (0, 2), (2, 0))


def with_halo(block, axis, width):
    count = lax.axis_size(axis)
    forward = [(i, i + 1) for i in range(count - 1)]
    backward = [(target, source) for source, target in forward]
    low = lax.ppermute(block[:, block.shape[1] - width :], axis, forward)
    high = lax.ppermute(block[:, :width], axis, backward)
    return jnp.concatenate([low, block, high], axis=1)


def passed_along(block, axis, distance):
    devices = range(lax.axis_size(axis))
    route = [((i - distance) % len(devices), i) for i in devices]
    return lax.ppermute(block, axis, route)


def split3(x):
    high = x.astype(jnp.bfloat16).astype(jnp.float32)
    rest = x - high
    mid = rest.astype(jnp.bfloat16).astype(jnp.float32)
    low = (rest - mid).astype(jnp.bfloat16).astype(jnp.float32)
    return high, mid, low


def kinematics(a0, along_x, along_y, along_z):
    softplus = jnp.maximum(a0, 0.0) + jnp.log1p(jnp.exp(-jnp.abs(a0)))
    hit_mass = mass_offset + softplus
    mass_sq = hit_mass * hit_mass
    trans_sq = along_x * along_x + along_y * along_y
    energy = jnp.sqrt(mass_sq + trans_sq + along_z * along_z)
    trans_mass = jnp.sqrt(mass_sq + trans_sq)
    magnitude = jnp.log((jnp.abs(along_z) + energy) / trans_mass)
    rapidity = jnp.where(along_z < 0.0, -magnitude, magnitude)
    inverse_pt = 1.0 / jnp.maximum(jnp.sqrt(trans_sq), floor_pt)
    return energy, mass_sq, rapidity, along_x * inverse_pt, along_y * inverse_pt, trans_sq


def raw_rows(block, head, at):
    raw = block[head, at : at + 4, :].astype(jnp.float32)
    return raw[0:1], raw[1:2], raw[2:3], raw[3:4]


def key_rows(raw, put):
    energy, mass_sq, rapidity, unit_x, unit_y, trans_sq = kinematics(*raw)
    one = jnp.ones_like(energy)
    rows = []
    parts = split3(energy)
    rows += [parts[a] for a, _ in PAIRS]
    rows += list(raw[1:])
    rows += list(split3(mass_sq)) + [one] * 3
    rows += list(split3(rapidity * rapidity)) + [one] * 3
    for value in (rapidity, unit_x, unit_y):
        parts = split3(value)
        rows += [parts[a] for a, _ in PAIRS]
    rows += [one, trans_sq]
    for offset, row in enumerate(rows):
        put(ROW_M + offset, row)


def query_rows(raw, put_m, put_d):
    energy, mass_sq, rapidity, unit_x, unit_y, trans_sq = kinematics(*raw)
    one = jnp.ones_like(energy)
    rows = []
    parts = split3(energy)
    rows += [2.0 * parts[b] for _, b in PAIRS]
    rows += [-2.0 * value for value in raw[1:]]
    rows += [one] * 3 + list(split3(mass_sq))
    for offset, row in enumerate(rows):
        put_m(ROW_M + offset, row)
    rows = [one] * 3 + list(split3(rapidity * rapidity))
    for value in (rapidity, unit_x, unit_y):
        parts = split3(value)
        rows += [-2.0 * parts[b] for _, b in PAIRS]
    rows += [2.0 * one]
    for offset, row in enumerate(rows):
        put_d(ROW_D + offset, row)
    return trans_sq


def attention_kernel(
    nblocks, chunk, tile, first, last,
    counts, pairw, own, *refs
):
    blocks, refs = refs[:nblocks], refs[nblocks:]
    if not first:
        state_in, refs = refs[:3], refs[3:]
    if last:
        out_ref, refs = refs[0], refs[1:]
    else:
        state_out, refs = refs[:3], refs[3:]
    feats, keys, key_ts, values, q_s, q_m, q_d, q_ts = refs
    rows = own.shape[2]
    head = pl.program_id(0)
    step = pl.program_id(1)

    @pl.when(step == 0)
    def prologue():
        lanes = lax.broadcasted_iota(jnp.int32, (1, rows), 1)
        zeros = jnp.zeros((DEPTH - ROW_MASK, rows), jnp.float32)
        scaled = own[head, 0:HD, :].astype(jnp.float32) * (LOG2E * HD**-0.5)
        high = scaled.astype(jnp.bfloat16).astype(jnp.float32)

        def put(row, value):
            feats[row : row + 1, :] = value

        feats[0:HD, :] = high
        feats[HD : 2 * HD, :] = scaled - high
        feats[2 * HD :, :] = zeros
        put(ROW_MASK, jnp.ones((1, rows), jnp.float32))
        q_s[...] = feats[...].astype(jnp.bfloat16)
        raw = raw_rows(own, head, 3 * HD)
        feats[...] = jnp.zeros((DEPTH, rows), jnp.float32)
        pending = []
        trans_sq = query_rows(raw, put, lambda row, value: pending.append((row, value)))
        q_m[...] = feats[...].astype(jnp.bfloat16)
        feats[...] = jnp.zeros((DEPTH, rows), jnp.float32)
        for row, value in pending:
            put(row, value)
        q_d[...] = feats[...].astype(jnp.bfloat16)
        q_ts[...] = jnp.broadcast_to(trans_sq, (8, rows))

        for index, block in enumerate(blocks):
            at = HD if block.shape[1] == PROJ else 0
            low = block[head, at : at + HD, :].astype(jnp.float32)
            feats[0:HD, :] = low
            feats[HD : 2 * HD, :] = low
            feats[2 * HD :, :] = zeros
            put(ROW_MASK, jnp.where(lanes < counts[index], 0.0, masked_score))
            key_rows(raw_rows(block, head, at + 2 * HD), put)
            turned = jnp.transpose(feats[...])
            start = index * rows
            keys[start : start + rows, :] = turned.astype(jnp.bfloat16)
            key_ts[start : start + rows, :] = jnp.broadcast_to(
                turned[:, ROW_TS : ROW_TS + 1], (rows, 128)
            )
            values[:, start : start + rows] = block[head, at + HD : at + 2 * HD, :]

    here = pl.multiple_of(step * tile, tile)
    cols = pl.ds(here, tile)
    rhs_s, rhs_m, rhs_d = q_s[:, cols], q_m[:, cols], q_d[:, cols]
    ts_query = q_ts[0:1, cols]
    w0, w1, w2 = pairw[head, 0], pairw[head, 1], pairw[head, 2]

    def one_chunk(base, index, carry):
        top, total, summed = carry
        at = pl.multiple_of(base + index * chunk, chunk)
        lhs = keys[pl.ds(at, chunk), :]
        dot = functools.partial(jnp.dot, preferred_element_type=jnp.float32)
        invariant = dot(lhs, rhs_m)
        separation = dot(lhs, rhs_d)
        ts_key = key_ts[pl.ds(at, chunk), :]
        ts_key = jnp.concatenate([ts_key] * (tile // 128), axis=1)
        kt_sq = jnp.minimum(ts_key, ts_query) * separation
        scores = dot(lhs, rhs_s) + w0 * jnp.log2(invariant)
        scores = scores + w1 * jnp.log2(1.0 + kt_sq) + w2 * jnp.log2(1.0 + separation)
        new_top = jnp.maximum(top, jnp.max(scores, axis=0, keepdims=True))
        fading = jnp.exp2(top - new_top)
        weights = jnp.exp2(scores - new_top)
        part = jnp.sum(weights.reshape(chunk // 8, 8, tile), axis=0)
        total = total * fading + part
        summed = summed * fading + dot(values[:, pl.ds(at, chunk)], weights.astype(jnp.bfloat16))
        return new_top, total, summed

    if first:
        carry = (
            jnp.full((1, tile), masked_score, jnp.float32),
            jnp.zeros((8, tile), jnp.float32),
            jnp.zeros((HD, tile), jnp.float32),
        )
    else:
        carry = tuple(ref[0, :, cols] for ref in state_in)

    def one_block(index, carry):
        count = (counts[index] + chunk - 1) // chunk
        return lax.fori_loop(0, count, functools.partial(one_chunk, index * rows), carry)

    carry = lax.fori_loop(0, nblocks, one_block, carry)
    if last:
        total = jnp.sum(carry[1], axis=0, keepdims=True)
        out_ref[:, cols] = (carry[2] / total).astype(jnp.bfloat16)
    else:
        for ref, value in zip(state_out, carry):
            ref[0, :, cols] = value


def attend(counts, pairw, own, blocks, state, last):
    heads, _, rows = own.shape
    nblocks = len(blocks)
    tile = 256
    chunk = 256
    whole = lambda array: pl.BlockSpec(array.shape, lambda h, q: (0,) * array.ndim)
    sizes = (1, 8, HD)
    state_specs = [pl.BlockSpec((1, size, rows), lambda h, q: (h, 0, 0)) for size in sizes]
    first = state is None
    operands = [counts, pairw, own, *blocks]
    smem = pl.BlockSpec(memory_space=pltpu.SMEM)
    in_specs = [smem, smem, whole(own)] + [whole(block) for block in blocks]
    if not first:
        operands += list(state)
        in_specs += state_specs
    if last:
        out_shape = jax.ShapeDtypeStruct((heads * HD, rows), jnp.bfloat16)
        out_specs = pl.BlockSpec((HD, rows), lambda h, q: (h, 0))
    else:
        out_shape = [jax.ShapeDtypeStruct((heads, size, rows), jnp.float32) for size in sizes]
        out_specs = state_specs
    pairs = heads * rows * nblocks * rows
    return pl.pallas_call(
        functools.partial(attention_kernel, nblocks, chunk, tile, first, last),
        grid=(heads, rows // tile),
        in_specs=in_specs,
        out_specs=out_specs,
        out_shape=out_shape,
        scratch_shapes=[
            pltpu.VMEM((DEPTH, rows), jnp.float32),
            pltpu.VMEM((nblocks * rows, DEPTH), jnp.bfloat16),
            pltpu.VMEM((nblocks * rows, 128), jnp.float32),
            pltpu.VMEM((HD, nblocks * rows), jnp.bfloat16),
            pltpu.VMEM((DEPTH, rows), jnp.bfloat16),
            pltpu.VMEM((DEPTH, rows), jnp.bfloat16),
            pltpu.VMEM((DEPTH, rows), jnp.bfloat16),
            pltpu.VMEM((8, rows), jnp.float32),
        ],
        compiler_params=pltpu.CompilerParams(vmem_limit_bytes=48 * 1024 * 1024),
        cost_estimate=pl.CostEstimate(
            flops=pairs * 2 * DEPTH * 4, bytes_accessed=1 << 20, transcendentals=4 * pairs
        ),
        name="attend_last" if last else "attend_own",
    )(*operands)


def shards(hit_features, depth_kernel, point_weight, pair_weight, hit_order, valid_counts):
    rows = hit_features.shape[1]
    heads_here = point_weight.shape[0] // PROJ
    position = jnp.arange(rows, dtype=jnp.int32)
    chosen = (position[:, None] == hit_order[None, :]).astype(jnp.bfloat16)
    ordered = jnp.dot(hit_features, chosen, preferred_element_type=jnp.float32)
    ordered = ordered.astype(jnp.bfloat16)
    half = KSIZE // 2
    padded = with_halo(ordered, "seq", half).astype(jnp.float32)
    taps = depth_kernel.astype(jnp.float32)
    summed = jnp.zeros((ordered.shape[0], rows), jnp.float32)
    for offset in range(KSIZE):
        summed = summed + taps[offset][:, None] * padded[:, offset : offset + rows]
    smoothed = summed.astype(jnp.bfloat16)
    projected = jnp.dot(
        point_weight,
        lax.all_gather(smoothed, "head", axis=0, tiled=True),
        preferred_element_type=jnp.float32,
    )
    stored = projected.reshape(heads_here, PROJ, rows).astype(jnp.bfloat16)
    travelling = stored[:, HD:]
    distances = (1, -1, -2)
    counts = [passed_along(valid_counts, "seq", distance) for distance in distances]
    arrived = [passed_along(travelling, "seq", distance) for distance in distances]
    state = attend(valid_counts, pair_weight, stored, [stored], None, False)
    return attend(jnp.concatenate(counts), pair_weight, stored, arrived, state, True)


def solution(mesh):
    in_specs = (
        P("head", ("groups", "seq")),
        P(None, "head"),
        P("head", None),
        P("head", None),
        P(("groups", "seq")),
        P(("groups", "seq")),
    )
    out_specs = P("head", ("groups", "seq"))
    return jax.shard_map(shards, mesh=mesh, in_specs=in_specs, out_specs=out_specs, check_vma=False)
```

```python
import functools

import jax
import jax.numpy as jnp
from jax import lax
from jax.experimental import pallas as pl
from jax.experimental.pallas import tpu as pltpu
from jax.sharding import PartitionSpec as P

HD = 32
KSIZE = 7
PROJ = 100

floor_pt = 0.1
mass_offset = 0.1
masked_score = -1e30
LOG2E = 1.4426950408889634

DEPTH = 128
ROW_M = 64
ROW_MASK = 79
ROW_D = 80
ROW_TS = 105

PAIRS = ((0, 0), (0, 1), (1, 0), (1, 1), (0, 2), (2, 0))


def with_halo(block, axis, width):
    count = lax.axis_size(axis)
    forward = [(i, i + 1) for i in range(count - 1)]
    backward = [(target, source) for source, target in forward]
    low = lax.ppermute(block[:, block.shape[1] - width :], axis, forward)
    high = lax.ppermute(block[:, :width], axis, backward)
    return jnp.concatenate([low, block, high], axis=1)


def passed_along(block, axis, distance):
    devices = range(lax.axis_size(axis))
    route = [((i - distance) % len(devices), i) for i in devices]
    return lax.ppermute(block, axis, route)


def split3(x):
    high = x.astype(jnp.bfloat16).astype(jnp.float32)
    rest = x - high
    mid = rest.astype(jnp.bfloat16).astype(jnp.float32)
    low = (rest - mid).astype(jnp.bfloat16).astype(jnp.float32)
    return high, mid, low


def kinematics(a0, along_x, along_y, along_z):
    softplus = jnp.maximum(a0, 0.0) + jnp.log1p(jnp.exp(-jnp.abs(a0)))
    hit_mass = mass_offset + softplus
    mass_sq = hit_mass * hit_mass
    trans_sq = along_x * along_x + along_y * along_y
    energy = jnp.sqrt(mass_sq + trans_sq + along_z * along_z)
    trans_mass = jnp.sqrt(mass_sq + trans_sq)
    magnitude = jnp.log((jnp.abs(along_z) + energy) / trans_mass)
    rapidity = jnp.where(along_z < 0.0, -magnitude, magnitude)
    inverse_pt = 1.0 / jnp.maximum(jnp.sqrt(trans_sq), floor_pt)
    return energy, mass_sq, rapidity, along_x * inverse_pt, along_y * inverse_pt, trans_sq


def key_rows(energy, mass_sq, rapidity, unit_x, unit_y, trans_sq, momentum):
    one = jnp.ones_like(energy)
    parts = split3(energy)
    rows = [parts[a] for a, _ in PAIRS]
    rows += momentum
    rows += list(split3(mass_sq)) + [one] * 3
    rows += [None]
    rows += list(split3(rapidity * rapidity)) + [one] * 3
    for value in (rapidity, unit_x, unit_y):
        parts = split3(value)
        rows += [parts[a] for a, _ in PAIRS]
    return rows + [one] + list(split3(trans_sq))


def query_rows(energy, mass_sq, rapidity, unit_x, unit_y, momentum):
    one = jnp.ones_like(energy)
    parts = split3(energy)
    rows = [2.0 * parts[b] for _, b in PAIRS]
    rows += [-2.0 * value for value in momentum]
    rows += [one] * 3 + list(split3(mass_sq))
    rows += [one]
    rows += [one] * 3 + list(split3(rapidity * rapidity))
    for value in (rapidity, unit_x, unit_y):
        parts = split3(value)
        rows += [-2.0 * parts[b] for _, b in PAIRS]
    return rows + [2.0 * one]


def attention_kernel(
    nblocks, chunk, tile, piece, first, last,
    counts, pairw, own, *refs
):
    if first:
        blocks = (own,)
    else:
        blocks, refs = refs[:nblocks], refs[nblocks:]
        state_in, refs = refs[:3], refs[3:]
    if last:
        out_ref, refs = refs[0], refs[1:]
    else:
        state_out, refs = refs[:3], refs[3:]
    feats, keys, key_ts, values, q_s, q_m, q_d, q_ts = refs
    rows = own.shape[2]
    head = pl.program_id(0)
    step = pl.program_id(1)
    dot = functools.partial(jnp.dot, preferred_element_type=jnp.float32)

    starts = [0]
    for index in range(nblocks):
        starts.append(starts[-1] + (counts[index] + 127) // 128 * 128)
    reached = starts[-1]

    @pl.when(step == 0)
    def prologue():
        lanes = lax.broadcasted_iota(jnp.int32, (1, rows), 1)
        sources = [(own, 3 * HD)]
        if not first:
            sources += [(block, 2 * HD) for block in blocks]
        raw = [ref[head, at : at + 4, :].astype(jnp.float32) for ref, at in sources]
        stacked = [jnp.concatenate([r[i : i + 1] for r in raw], axis=0) for i in range(4)]
        kin = kinematics(*stacked)
        own_rows = query_rows(*[value[0:1] for value in kin[:5]], [v[0:1] for v in stacked[1:]])
        keyed = key_rows(*kin, stacked[1:])
        q_ts[...] = jnp.broadcast_to(kin[5][0:1], (8, rows))

        scaled = own[head, 0:HD, :].astype(jnp.float32) * (LOG2E * HD**-0.5)
        high = scaled.astype(jnp.bfloat16).astype(jnp.float32)
        feats[0:HD, :] = high
        feats[HD : 2 * HD, :] = scaled - high
        feats[ROW_TS - 1 :, :] = jnp.zeros((DEPTH - ROW_TS + 1, rows), jnp.float32)
        for offset, row in enumerate(own_rows):
            feats[ROW_M + offset : ROW_M + offset + 1, :] = row
        both = feats[...]
        at_row = lax.broadcasted_iota(jnp.int32, (DEPTH, rows), 0)
        in_m = (at_row >= ROW_M) & (at_row < ROW_MASK)
        in_s = (at_row < ROW_M) | (at_row == ROW_MASK)
        q_s[...] = jnp.where(in_s, both, 0.0).astype(jnp.bfloat16)
        q_m[...] = jnp.where(in_m, both, 0.0).astype(jnp.bfloat16)
        q_d[...] = jnp.where(at_row >= ROW_D, both, 0.0).astype(jnp.bfloat16)

        feat_row = lax.broadcasted_iota(jnp.int32, (DEPTH, 128), 0)
        pick = (feat_row >= ROW_TS) & (feat_row < ROW_TS + 3)
        pick = jnp.where(pick, 1.0, 0.0).astype(jnp.bfloat16)
        for index, block in enumerate(blocks):
            at = HD if first else 0
            low = block[head, at : at + HD, :].astype(jnp.float32)
            feats[0:HD, :] = low
            feats[HD : 2 * HD, :] = low
            which = index if first else index + 1
            for offset, row in enumerate(keyed):
                if row is None:
                    value = jnp.where(lanes < counts[index], 0.0, masked_score)
                else:
                    value = row[which : which + 1]
                feats[ROW_M + offset : ROW_M + offset + 1, :] = value
            turned = jnp.transpose(feats[...].astype(jnp.bfloat16))
            start = pl.multiple_of(starts[index], 128)
            keys[pl.ds(start, rows), :] = turned
            key_ts[pl.ds(start, rows), :] = dot(turned, pick)
            values[:, pl.ds(start, rows)] = block[head, at + HD : at + 2 * HD, :]
        start = pl.multiple_of(reached, 128)
        lane = lax.broadcasted_iota(jnp.int32, (chunk, DEPTH), 1)
        empty = jnp.where(lane == ROW_MASK, masked_score, jnp.where(lane == ROW_M + 9, 1.0, 0.0))
        keys[pl.ds(start, chunk), :] = empty.astype(jnp.bfloat16)
        key_ts[pl.ds(start, chunk), :] = jnp.zeros((chunk, 128), jnp.float32)
        values[:, pl.ds(start, chunk)] = jnp.zeros((HD, chunk), jnp.bfloat16)

    here = pl.multiple_of(step * tile, tile)
    w0, w1, w2 = [pairw[head, i] * LOG2E for i in range(3)]
    cols = [pl.ds(pl.multiple_of(here + lo, piece), piece) for lo in range(0, tile, piece)]

    def one_chunk(index, carry):
        at = pl.multiple_of(index * chunk, chunk)

        def score(part):
            col = cols[part]
            best = carry[part][0]
            ts_query = q_ts[0:1, col]
            scores = []
            for offset in range(0, chunk, 256):
                some = pl.ds(at + offset, 256)
                lhs = keys[some, :]
                invariant = dot(lhs, q_m[:, col])
                separation = dot(lhs, q_d[:, col])
                ts_key = jnp.concatenate([key_ts[some, :]] * (piece // 128), axis=1)
                kt_sq = jnp.minimum(ts_key, ts_query) * separation
                score = dot(lhs, q_s[:, col]) + w0 * jnp.log(invariant)
                score = score + w1 * jnp.log(1.0 + kt_sq) + w2 * jnp.log(1.0 + separation)
                best = jnp.maximum(best, jnp.max(score, axis=0, keepdims=True))
                scores.append(score)
            return best, scores

        def weigh(part, best, scores):
            top, total, summed = carry[part]
            fading = jnp.exp2(top - best)
            total = total * fading
            summed = summed * fading
            for number, score in enumerate(scores):
                weights = jnp.exp2(score - best)
                total = total + jnp.sum(weights.reshape(256 // 8, 8, piece), axis=0)
                some = pl.ds(at + number * 256, 256)
                summed = summed + dot(values[:, some], weights.astype(jnp.bfloat16))
            return best, total, summed

        done = []
        waiting = score(0)
        for part in range(1, len(cols)):
            following = score(part)
            done.append(weigh(part - 1, *waiting))
            waiting = following
        done.append(weigh(len(cols) - 1, *waiting))
        return tuple(done)

    if first:
        carry = tuple(
            (
                jnp.full((1, piece), masked_score, jnp.float32),
                jnp.zeros((8, piece), jnp.float32),
                jnp.zeros((HD, piece), jnp.float32),
            )
            for _ in cols
        )
    else:
        carry = tuple(tuple(ref[0, :, col] for ref in state_in) for col in cols)
    carry = lax.fori_loop(0, (reached + chunk - 1) // chunk, one_chunk, carry)
    for col, (top, total, summed) in zip(cols, carry):
        if last:
            total = jnp.sum(total, axis=0, keepdims=True)
            out_ref[:, col] = (summed / total).astype(jnp.bfloat16)
        else:
            for ref, value in zip(state_out, (top, total, summed)):
                ref[0, :, col] = value


def attend(counts, pairw, own, blocks, state, last):
    heads, _, rows = own.shape
    nblocks = len(blocks)
    tile = rows
    chunk = 512
    piece = 256
    held = nblocks * rows + chunk
    whole = lambda array: pl.BlockSpec(array.shape, lambda h, q: (0,) * array.ndim)
    sizes = (1, 8, HD)
    state_specs = [pl.BlockSpec((1, size, rows), lambda h, q: (h, 0, 0)) for size in sizes]
    first = state is None
    operands = [counts, pairw, own, *([] if first else blocks)]
    smem = pl.BlockSpec(memory_space=pltpu.SMEM)
    in_specs = [smem, smem, whole(own)] + [whole(block) for block in operands[3:]]
    if not first:
        operands += list(state)
        in_specs += state_specs
    if last:
        out_shape = jax.ShapeDtypeStruct((heads * HD, rows), jnp.bfloat16)
        out_specs = pl.BlockSpec((HD, rows), lambda h, q: (h, 0))
    else:
        out_shape = [jax.ShapeDtypeStruct((heads, size, rows), jnp.float32) for size in sizes]
        out_specs = state_specs
    pairs = heads * rows * nblocks * rows
    return pl.pallas_call(
        functools.partial(attention_kernel, nblocks, chunk, tile, piece, first, last),
        grid=(heads, rows // tile),
        in_specs=in_specs,
        out_specs=out_specs,
        out_shape=out_shape,
        scratch_shapes=[
            pltpu.VMEM((DEPTH, rows), jnp.float32),
            pltpu.VMEM((held, DEPTH), jnp.bfloat16),
            pltpu.VMEM((held, 128), jnp.float32),
            pltpu.VMEM((HD, held), jnp.bfloat16),
            pltpu.VMEM((DEPTH, rows), jnp.bfloat16),
            pltpu.VMEM((DEPTH, rows), jnp.bfloat16),
            pltpu.VMEM((DEPTH, rows), jnp.bfloat16),
            pltpu.VMEM((8, rows), jnp.float32),
        ],
        compiler_params=pltpu.CompilerParams(vmem_limit_bytes=48 * 1024 * 1024),
        cost_estimate=pl.CostEstimate(
            flops=pairs * 2 * DEPTH * 4, bytes_accessed=1 << 20, transcendentals=4 * pairs
        ),
        name="attend_last" if last else "attend_own",
    )(*operands)


def shards(hit_features, depth_kernel, point_weight, pair_weight, hit_order, valid_counts):
    rows = hit_features.shape[1]
    heads_here = point_weight.shape[0] // PROJ
    position = jnp.arange(rows, dtype=jnp.int32)
    chosen = (position[:, None] == hit_order[None, :]).astype(jnp.bfloat16)
    ordered = jnp.dot(hit_features, chosen, preferred_element_type=jnp.float32)
    ordered = ordered.astype(jnp.bfloat16)
    half = KSIZE // 2
    padded = with_halo(ordered, "seq", half).astype(jnp.float32)
    taps = depth_kernel.astype(jnp.float32)
    summed = jnp.zeros((ordered.shape[0], rows), jnp.float32)
    for offset in range(KSIZE):
        summed = summed + taps[offset][:, None] * padded[:, offset : offset + rows]
    smoothed = summed.astype(jnp.bfloat16)
    projected = jnp.dot(
        point_weight,
        lax.all_gather(smoothed, "head", axis=0, tiled=True),
        preferred_element_type=jnp.float32,
    )
    stored = projected.reshape(heads_here, PROJ, rows).astype(jnp.bfloat16)
    travelling = stored[:, HD:]
    distances = (1, -1, -2)
    counts = [passed_along(valid_counts, "seq", distance) for distance in distances]
    arrived = [passed_along(travelling, "seq", distance) for distance in distances]
    state = attend(valid_counts, pair_weight, stored, [stored], None, False)
    return attend(jnp.concatenate(counts), pair_weight, stored, arrived, state, True)


def solution(mesh):
    in_specs = (
        P("head", ("groups", "seq")),
        P(None, "head"),
        P("head", None),
        P("head", None),
        P(("groups", "seq")),
        P(("groups", "seq")),
    )
    out_specs = P("head", ("groups", "seq"))
    return jax.shard_map(shards, mesh=mesh, in_specs=in_specs, out_specs=out_specs, check_vma=False)
```

```python
import functools

import jax
import jax.numpy as jnp
from jax import lax
from jax.experimental import pallas as pl
from jax.experimental.pallas import tpu as pltpu
from jax.sharding import PartitionSpec as P

HD = 32
KSIZE = 7
PROJ = 100

floor_pt = 0.1
mass_offset = 0.1
masked_score = -1e30
LOG2E = 1.4426950408889634

DEPTH = 128
ROW_M = 64
ROW_MASK = 79
ROW_D = 80
ROW_TS = 105

PAIRS = ((0, 0), (0, 1), (1, 0), (1, 1), (0, 2), (2, 0))


def halo(start, end, axis):
    count = lax.axis_size(axis)
    forward = [(i, i + 1) for i in range(count - 1)]
    backward = [(target, source) for source, target in forward]
    return lax.ppermute(end, axis, forward), lax.ppermute(start, axis, backward)


def passed_along(block, axis, distance):
    devices = range(lax.axis_size(axis))
    route = [((i - distance) % len(devices), i) for i in devices]
    return lax.ppermute(block, axis, route)


def split3(x):
    high = x.astype(jnp.bfloat16).astype(jnp.float32)
    rest = x - high
    mid = rest.astype(jnp.bfloat16).astype(jnp.float32)
    low = (rest - mid).astype(jnp.bfloat16).astype(jnp.float32)
    return high, mid, low


def kinematics(a0, along_x, along_y, along_z):
    softplus = jnp.maximum(a0, 0.0) + jnp.log1p(jnp.exp(-jnp.abs(a0)))
    hit_mass = mass_offset + softplus
    mass_sq = hit_mass * hit_mass
    trans_sq = along_x * along_x + along_y * along_y
    energy = jnp.sqrt(mass_sq + trans_sq + along_z * along_z)
    trans_mass = jnp.sqrt(mass_sq + trans_sq)
    magnitude = jnp.log((jnp.abs(along_z) + energy) / trans_mass)
    rapidity = jnp.where(along_z < 0.0, -magnitude, magnitude)
    inverse_pt = 1.0 / jnp.maximum(jnp.sqrt(trans_sq), floor_pt)
    return energy, mass_sq, rapidity, along_x * inverse_pt, along_y * inverse_pt, trans_sq


def key_rows(energy, mass_sq, rapidity, unit_x, unit_y, trans_sq, momentum):
    one = jnp.ones_like(energy)
    parts = split3(energy)
    rows = [parts[a] for a, _ in PAIRS]
    rows += momentum
    rows += list(split3(mass_sq)) + [one] * 3
    rows += [None]
    rows += list(split3(rapidity * rapidity)) + [one] * 3
    for value in (rapidity, unit_x, unit_y):
        parts = split3(value)
        rows += [parts[a] for a, _ in PAIRS]
    return rows + [one] + list(split3(trans_sq))


def query_rows(energy, mass_sq, rapidity, unit_x, unit_y, momentum):
    one = jnp.ones_like(energy)
    parts = split3(energy)
    rows = [2.0 * parts[b] for _, b in PAIRS]
    rows += [-2.0 * value for value in momentum]
    rows += [one] * 3 + list(split3(mass_sq))
    rows += [one]
    rows += [one] * 3 + list(split3(rapidity * rapidity))
    for value in (rapidity, unit_x, unit_y):
        parts = split3(value)
        rows += [-2.0 * parts[b] for _, b in PAIRS]
    return rows + [2.0 * one]


def attention_kernel(
    nblocks, chunk, tile, piece, first, last,
    counts, places, pairw, own, *refs
):
    if first:
        blocks = [own.at[:, HD:, :]]
    else:
        arrived, refs = refs[0], refs[1:]
        blocks = [arrived.at[places[index]] for index in range(nblocks)]
        state_in, refs = refs[:3], refs[3:]
    if last:
        out_ref, refs = refs[0], refs[1:]
    else:
        state_out, refs = refs[:3], refs[3:]
    feats, keys, key_ts, values, q_s, q_m, q_d, q_ts = refs
    rows = own.shape[2]
    head = pl.program_id(0)
    step = pl.program_id(1)
    dot = functools.partial(jnp.dot, preferred_element_type=jnp.float32)

    starts = [0]
    for index in range(nblocks):
        starts.append(starts[-1] + (counts[index] + 127) // 128 * 128)
    reached = starts[-1]

    @pl.when(step == 0)
    def prologue():
        lanes = lax.broadcasted_iota(jnp.int32, (1, rows), 1)
        sources = [(own, 3 * HD)]
        if not first:
            sources += [(block, 2 * HD) for block in blocks]
        raw = [ref[head, at : at + 4, :].astype(jnp.float32) for ref, at in sources]
        stacked = [jnp.concatenate([r[i : i + 1] for r in raw], axis=0) for i in range(4)]
        kin = kinematics(*stacked)
        own_rows = query_rows(*[value[0:1] for value in kin[:5]], [v[0:1] for v in stacked[1:]])
        keyed = key_rows(*kin, stacked[1:])
        q_ts[...] = jnp.broadcast_to(kin[5][0:1], (8, rows))

        scaled = own[head, 0:HD, :].astype(jnp.float32) * (LOG2E * HD**-0.5)
        high = scaled.astype(jnp.bfloat16).astype(jnp.float32)
        feats[0:HD, :] = high
        feats[HD : 2 * HD, :] = scaled - high
        feats[ROW_TS - 1 :, :] = jnp.zeros((DEPTH - ROW_TS + 1, rows), jnp.float32)
        for offset, row in enumerate(own_rows):
            feats[ROW_M + offset : ROW_M + offset + 1, :] = row
        both = feats[...]
        at_row = lax.broadcasted_iota(jnp.int32, (DEPTH, rows), 0)
        in_m = (at_row >= ROW_M) & (at_row < ROW_MASK)
        in_s = (at_row < ROW_M) | (at_row == ROW_MASK)
        q_s[...] = jnp.where(in_s, both, 0.0).astype(jnp.bfloat16)
        q_m[...] = jnp.where(in_m, both, 0.0).astype(jnp.bfloat16)
        q_d[...] = jnp.where(at_row >= ROW_D, both, 0.0).astype(jnp.bfloat16)

        feat_row = lax.broadcasted_iota(jnp.int32, (DEPTH, 128), 0)
        pick = (feat_row >= ROW_TS) & (feat_row < ROW_TS + 3)
        pick = jnp.where(pick, 1.0, 0.0).astype(jnp.bfloat16)
        for index, block in enumerate(blocks):
            low = block[head, 0:HD, :].astype(jnp.float32)
            feats[0:HD, :] = low
            feats[HD : 2 * HD, :] = low
            which = index if first else index + 1
            for offset, row in enumerate(keyed):
                if row is None:
                    value = jnp.where(lanes < counts[index], 0.0, masked_score)
                else:
                    value = row[which : which + 1]
                feats[ROW_M + offset : ROW_M + offset + 1, :] = value
            turned = jnp.transpose(feats[...].astype(jnp.bfloat16))
            start = pl.multiple_of(starts[index], 128)
            keys[pl.ds(start, rows), :] = turned
            key_ts[pl.ds(start, rows), :] = dot(turned, pick)
            values[:, pl.ds(start, rows)] = block[head, HD : 2 * HD, :]
        start = pl.multiple_of(reached, 128)
        lane = lax.broadcasted_iota(jnp.int32, (chunk, DEPTH), 1)
        empty = jnp.where(lane == ROW_MASK, masked_score, jnp.where(lane == ROW_M + 9, 1.0, 0.0))
        keys[pl.ds(start, chunk), :] = empty.astype(jnp.bfloat16)
        key_ts[pl.ds(start, chunk), :] = jnp.zeros((chunk, 128), jnp.float32)
        values[:, pl.ds(start, chunk)] = jnp.zeros((HD, chunk), jnp.bfloat16)

    here = pl.multiple_of(step * tile, tile)
    w0, w1, w2 = [pairw[head, i] * LOG2E for i in range(3)]
    cols = [pl.ds(pl.multiple_of(here + lo, piece), piece) for lo in range(0, tile, piece)]

    def one_chunk(index, carry):
        at = pl.multiple_of(index * chunk, chunk)

        def score(part):
            col = cols[part]
            best = carry[part][0]
            ts_query = q_ts[0:1, col]
            scores = []
            for offset in range(0, chunk, 256):
                some = pl.ds(at + offset, 256)
                lhs = keys[some, :]
                invariant = dot(lhs, q_m[:, col])
                separation = dot(lhs, q_d[:, col])
                ts_key = jnp.concatenate([key_ts[some, :]] * (piece // 128), axis=1)
                kt_sq = jnp.minimum(ts_key, ts_query) * separation
                score = dot(lhs, q_s[:, col]) + w0 * jnp.log(invariant)
                score = score + w1 * jnp.log(1.0 + kt_sq) + w2 * jnp.log(1.0 + separation)
                best = jnp.maximum(best, jnp.max(score, axis=0, keepdims=True))
                scores.append(score)
            return best, scores

        def weigh(part, best, scores):
            top, total, summed = carry[part]
            fading = jnp.exp2(top - best)
            total = total * fading
            summed = summed * fading
            for number, score in enumerate(scores):
                weights = jnp.exp2(score - best)
                total = total + jnp.sum(weights.reshape(256 // 8, 8, piece), axis=0)
                some = pl.ds(at + number * 256, 256)
                summed = summed + dot(values[:, some], weights.astype(jnp.bfloat16))
            return best, total, summed

        done = []
        waiting = score(0)
        for part in range(1, len(cols)):
            following = score(part)
            done.append(weigh(part - 1, *waiting))
            waiting = following
        done.append(weigh(len(cols) - 1, *waiting))
        return tuple(done)

    if first:
        carry = tuple(
            (
                jnp.full((1, piece), masked_score, jnp.float32),
                jnp.zeros((8, piece), jnp.float32),
                jnp.zeros((HD, piece), jnp.float32),
            )
            for _ in cols
        )
    else:
        carry = tuple(tuple(ref[0, :, col] for ref in state_in) for col in cols)
    carry = lax.fori_loop(0, (reached + chunk - 1) // chunk, one_chunk, carry)
    for col, (top, total, summed) in zip(cols, carry):
        if last:
            total = jnp.sum(total, axis=0, keepdims=True)
            out_ref[:, col] = (summed / total).astype(jnp.bfloat16)
        else:
            for ref, value in zip(state_out, (top, total, summed)):
                ref[0, :, col] = value


def attend(counts, places, pairw, own, arrived, state, last):
    heads, _, rows = own.shape
    nblocks = counts.shape[0]
    tile = rows
    chunk = 512
    piece = 256
    held = nblocks * rows + chunk
    whole = lambda array: pl.BlockSpec(array.shape, lambda h, q: (0,) * array.ndim)
    sizes = (1, 8, HD)
    state_specs = [pl.BlockSpec((1, size, rows), lambda h, q: (h, 0, 0)) for size in sizes]
    first = state is None
    operands = [counts, places, pairw, own]
    smem = pl.BlockSpec(memory_space=pltpu.SMEM)
    in_specs = [smem, smem, smem, whole(own)]
    if not first:
        operands += [arrived, *state]
        in_specs += [whole(arrived), *state_specs]
    if last:
        out_shape = jax.ShapeDtypeStruct((heads * HD, rows), jnp.bfloat16)
        out_specs = pl.BlockSpec((HD, rows), lambda h, q: (h, 0))
    else:
        out_shape = [jax.ShapeDtypeStruct((heads, size, rows), jnp.float32) for size in sizes]
        out_specs = state_specs
    pairs = heads * rows * nblocks * rows
    return pl.pallas_call(
        functools.partial(attention_kernel, nblocks, chunk, tile, piece, first, last),
        grid=(heads, rows // tile),
        in_specs=in_specs,
        out_specs=out_specs,
        out_shape=out_shape,
        scratch_shapes=[
            pltpu.VMEM((DEPTH, rows), jnp.float32),
            pltpu.VMEM((held, DEPTH), jnp.bfloat16),
            pltpu.VMEM((held, 128), jnp.float32),
            pltpu.VMEM((HD, held), jnp.bfloat16),
            pltpu.VMEM((DEPTH, rows), jnp.bfloat16),
            pltpu.VMEM((DEPTH, rows), jnp.bfloat16),
            pltpu.VMEM((DEPTH, rows), jnp.bfloat16),
            pltpu.VMEM((8, rows), jnp.float32),
        ],
        compiler_params=pltpu.CompilerParams(vmem_limit_bytes=48 * 1024 * 1024),
        cost_estimate=pl.CostEstimate(
            flops=pairs * 2 * DEPTH * 4, bytes_accessed=1 << 20, transcendentals=4 * pairs
        ),
        name="attend_last" if last else "attend_own",
    )(*operands)


def shards(hit_features, depth_kernel, point_weight, pair_weight, hit_order, valid_counts):
    rows = hit_features.shape[1]
    heads_here = point_weight.shape[0] // PROJ
    half = KSIZE // 2
    position = jnp.arange(rows, dtype=jnp.int32)

    def picked(order):
        chosen = (position[:, None] == order[None, :]).astype(jnp.bfloat16)
        found = jnp.dot(hit_features, chosen, preferred_element_type=jnp.float32)
        return found.astype(jnp.bfloat16)

    edges = picked(jnp.concatenate([hit_order[:half], hit_order[rows - half :]]))
    low, high = halo(edges[:, :half], edges[:, half:], "seq")
    distances = (1, -1, -2)
    counts = jnp.concatenate([passed_along(valid_counts, "seq", d) for d in distances])
    low, high, counts = lax.optimization_barrier((low, high, counts))
    padded = jnp.concatenate([low, picked(hit_order), high], axis=1).astype(jnp.float32)
    taps = depth_kernel.astype(jnp.float32)
    summed = jnp.zeros((padded.shape[0], rows), jnp.float32)
    for offset in range(KSIZE):
        summed = summed + taps[offset][:, None] * padded[:, offset : offset + rows]
    smoothed = summed.astype(jnp.bfloat16)
    projected = jnp.dot(
        point_weight,
        lax.all_gather(smoothed, "head", axis=0, tiled=True),
        preferred_element_type=jnp.float32,
    )
    stored = projected.reshape(heads_here, PROJ, rows).astype(jnp.bfloat16)
    travelling = stored[:, HD:]
    total = lax.axis_size("seq")
    if total == len(distances) + 1:
        arrived = lax.all_gather(travelling, "seq", axis=0)
        places = (lax.axis_index("seq") - jnp.array(distances, jnp.int32)) % total
    else:
        arrived = jnp.stack([passed_along(travelling, "seq", d) for d in distances])
        places = jnp.arange(len(distances), dtype=jnp.int32)
    state = attend(valid_counts, places, pair_weight, stored, None, None, False)
    return attend(counts, places, pair_weight, stored, arrived, state, True)


def solution(mesh):
    in_specs = (
        P("head", ("groups", "seq")),
        P(None, "head"),
        P("head", None),
        P("head", None),
        P(("groups", "seq")),
        P(("groups", "seq")),
    )
    out_specs = P("head", ("groups", "seq"))
    return jax.shard_map(shards, mesh=mesh, in_specs=in_specs, out_specs=out_specs, check_vma=False)
```

```python
import functools

import jax
import jax.numpy as jnp
from jax import lax
from jax.experimental import pallas as pl
from jax.experimental.pallas import tpu as pltpu
from jax.sharding import PartitionSpec as P

HD = 32
KSIZE = 7
PROJ = 100

floor_pt = 0.1
mass_offset = 0.1
masked_score = -1e30
LOG2E = 1.4426950408889634

DEPTH = 128
ROW_M = 64
ROW_MASK = 79
ROW_D = 80
ROW_TS = 105

PAIRS = ((0, 0), (0, 1), (1, 0), (1, 1), (0, 2), (2, 0))


def with_halo(block, axis, width):
    count = lax.axis_size(axis)
    forward = [(i, i + 1) for i in range(count - 1)]
    backward = [(target, source) for source, target in forward]
    low = lax.ppermute(block[:, block.shape[1] - width :], axis, forward)
    high = lax.ppermute(block[:, :width], axis, backward)
    return jnp.concatenate([low, block, high], axis=1)


def passed_along(block, axis, distance):
    devices = range(lax.axis_size(axis))
    route = [((i - distance) % len(devices), i) for i in devices]
    return lax.ppermute(block, axis, route)


def split3(x):
    high = x.astype(jnp.bfloat16).astype(jnp.float32)
    rest = x - high
    mid = rest.astype(jnp.bfloat16).astype(jnp.float32)
    low = (rest - mid).astype(jnp.bfloat16).astype(jnp.float32)
    return high, mid, low


def kinematics(a0, along_x, along_y, along_z):
    softplus = jnp.maximum(a0, 0.0) + jnp.log1p(jnp.exp(-jnp.abs(a0)))
    hit_mass = mass_offset + softplus
    mass_sq = hit_mass * hit_mass
    trans_sq = along_x * along_x + along_y * along_y
    energy = jnp.sqrt(mass_sq + trans_sq + along_z * along_z)
    trans_mass = jnp.sqrt(mass_sq + trans_sq)
    magnitude = jnp.log((jnp.abs(along_z) + energy) / trans_mass)
    rapidity = jnp.where(along_z < 0.0, -magnitude, magnitude)
    inverse_pt = 1.0 / jnp.maximum(jnp.sqrt(trans_sq), floor_pt)
    return energy, mass_sq, rapidity, along_x * inverse_pt, along_y * inverse_pt, trans_sq


def key_rows(energy, mass_sq, rapidity, unit_x, unit_y, trans_sq, momentum):
    one = jnp.ones_like(energy)
    parts = split3(energy)
    rows = [parts[a] for a, _ in PAIRS]
    rows += momentum
    rows += list(split3(mass_sq)) + [one] * 3
    rows += [None]
    rows += list(split3(rapidity * rapidity)) + [one] * 3
    for value in (rapidity, unit_x, unit_y):
        parts = split3(value)
        rows += [parts[a] for a, _ in PAIRS]
    return rows + [one] + list(split3(trans_sq))


def query_rows(energy, mass_sq, rapidity, unit_x, unit_y, momentum):
    one = jnp.ones_like(energy)
    parts = split3(energy)
    rows = [2.0 * parts[b] for _, b in PAIRS]
    rows += [-2.0 * value for value in momentum]
    rows += [one] * 3 + list(split3(mass_sq))
    rows += [one]
    rows += [one] * 3 + list(split3(rapidity * rapidity))
    for value in (rapidity, unit_x, unit_y):
        parts = split3(value)
        rows += [-2.0 * parts[b] for _, b in PAIRS]
    return rows + [2.0 * one]


def attention_kernel(
    nblocks, chunk, tile, piece, first, last,
    counts, pairw, own, *refs
):
    if first:
        blocks = (own,)
    else:
        blocks, refs = refs[:nblocks], refs[nblocks:]
        state_in, refs = refs[:3], refs[3:]
    if last:
        out_ref, refs = refs[0], refs[1:]
    else:
        state_out, refs = refs[:3], refs[3:]
    feats, keys, key_ts, values, q_s, q_m, q_d, q_ts = refs
    rows = own.shape[2]
    head = pl.program_id(0)
    step = pl.program_id(1)
    dot = functools.partial(jnp.dot, preferred_element_type=jnp.float32)

    starts = [0]
    for index in range(nblocks):
        starts.append(starts[-1] + (counts[index] + 127) // 128 * 128)
    reached = starts[-1]

    @pl.when(step == 0)
    def prologue():
        lanes = lax.broadcasted_iota(jnp.int32, (1, rows), 1)
        sources = [(own, 3 * HD)]
        if not first:
            sources += [(block, 2 * HD) for block in blocks]
        raw = [ref[head, at : at + 4, :].astype(jnp.float32) for ref, at in sources]
        stacked = [jnp.concatenate([r[i : i + 1] for r in raw], axis=0) for i in range(4)]
        kin = kinematics(*stacked)
        own_rows = query_rows(*[value[0:1] for value in kin[:5]], [v[0:1] for v in stacked[1:]])
        keyed = key_rows(*kin, stacked[1:])
        q_ts[...] = jnp.broadcast_to(kin[5][0:1], (8, rows))

        scaled = own[head, 0:HD, :].astype(jnp.float32) * (LOG2E * HD**-0.5)
        high = scaled.astype(jnp.bfloat16).astype(jnp.float32)
        feats[0:HD, :] = high
        feats[HD : 2 * HD, :] = scaled - high
        feats[ROW_TS - 1 :, :] = jnp.zeros((DEPTH - ROW_TS + 1, rows), jnp.float32)
        for offset, row in enumerate(own_rows):
            feats[ROW_M + offset : ROW_M + offset + 1, :] = row
        both = feats[...]
        at_row = lax.broadcasted_iota(jnp.int32, (DEPTH, rows), 0)
        in_m = (at_row >= ROW_M) & (at_row < ROW_MASK)
        in_s = (at_row < ROW_M) | (at_row == ROW_MASK)
        q_s[...] = jnp.where(in_s, both, 0.0).astype(jnp.bfloat16)
        q_m[...] = jnp.where(in_m, both, 0.0).astype(jnp.bfloat16)
        q_d[...] = jnp.where(at_row >= ROW_D, both, 0.0).astype(jnp.bfloat16)

        feat_row = lax.broadcasted_iota(jnp.int32, (DEPTH, 128), 0)
        pick = (feat_row >= ROW_TS) & (feat_row < ROW_TS + 3)
        pick = jnp.where(pick, 1.0, 0.0).astype(jnp.bfloat16)
        for index, block in enumerate(blocks):
            at = HD if first else 0
            low = block[head, at : at + HD, :].astype(jnp.float32)
            feats[0:HD, :] = low
            feats[HD : 2 * HD, :] = low
            which = index if first else index + 1
            for offset, row in enumerate(keyed):
                if row is None:
                    value = jnp.where(lanes < counts[index], 0.0, masked_score)
                else:
                    value = row[which : which + 1]
                feats[ROW_M + offset : ROW_M + offset + 1, :] = value
            turned = jnp.transpose(feats[...].astype(jnp.bfloat16))
            start = pl.multiple_of(starts[index], 128)
            keys[pl.ds(start, rows), :] = turned
            key_ts[pl.ds(start, rows), :] = dot(turned, pick)
            values[:, pl.ds(start, rows)] = block[head, at + HD : at + 2 * HD, :]
        start = pl.multiple_of(reached, 128)
        lane = lax.broadcasted_iota(jnp.int32, (chunk, DEPTH), 1)
        empty = jnp.where(lane == ROW_MASK, masked_score, jnp.where(lane == ROW_M + 9, 1.0, 0.0))
        keys[pl.ds(start, chunk), :] = empty.astype(jnp.bfloat16)
        key_ts[pl.ds(start, chunk), :] = jnp.zeros((chunk, 128), jnp.float32)
        values[:, pl.ds(start, chunk)] = jnp.zeros((HD, chunk), jnp.bfloat16)

    here = pl.multiple_of(step * tile, tile)
    w0, w1, w2 = [pairw[head, i] * LOG2E for i in range(3)]
    cols = [pl.ds(pl.multiple_of(here + lo, piece), piece) for lo in range(0, tile, piece)]

    def one_chunk(index, carry):
        at = pl.multiple_of(index * chunk, chunk)

        def score(part):
            col = cols[part]
            best = carry[part][0]
            ts_query = q_ts[0:1, col]
            scores = []
            for offset in range(0, chunk, 256):
                some = pl.ds(at + offset, 256)
                lhs = keys[some, :]
                invariant = dot(lhs, q_m[:, col])
                separation = dot(lhs, q_d[:, col])
                ts_key = jnp.concatenate([key_ts[some, :]] * (piece // 128), axis=1)
                kt_sq = jnp.minimum(ts_key, ts_query) * separation
                score = dot(lhs, q_s[:, col]) + w0 * jnp.log(invariant)
                score = score + w1 * jnp.log(1.0 + kt_sq) + w2 * jnp.log(1.0 + separation)
                best = jnp.maximum(best, jnp.max(score, axis=0, keepdims=True))
                scores.append(score)
            return best, scores

        def weigh(part, best, scores):
            top, total, summed = carry[part]
            fading = jnp.exp2(top - best)
            total = total * fading
            summed = summed * fading
            for number, score in enumerate(scores):
                weights = jnp.exp2(score - best)
                total = total + jnp.sum(weights.reshape(256 // 8, 8, piece), axis=0)
                some = pl.ds(at + number * 256, 256)
                summed = summed + dot(values[:, some], weights.astype(jnp.bfloat16))
            return best, total, summed

        done = []
        waiting = score(0)
        for part in range(1, len(cols)):
            following = score(part)
            done.append(weigh(part - 1, *waiting))
            waiting = following
        done.append(weigh(len(cols) - 1, *waiting))
        return tuple(done)

    if first:
        carry = tuple(
            (
                jnp.full((1, piece), masked_score, jnp.float32),
                jnp.zeros((8, piece), jnp.float32),
                jnp.zeros((HD, piece), jnp.float32),
            )
            for _ in cols
        )
    else:
        carry = tuple(tuple(ref[0, :, col] for ref in state_in) for col in cols)
    carry = lax.fori_loop(0, (reached + chunk - 1) // chunk, one_chunk, carry)
    for col, (top, total, summed) in zip(cols, carry):
        if last:
            total = jnp.sum(total, axis=0, keepdims=True)
            out_ref[:, col] = (summed / total).astype(jnp.bfloat16)
        else:
            for ref, value in zip(state_out, (top, total, summed)):
                ref[0, :, col] = value


def attend(counts, pairw, own, blocks, state, last):
    heads, _, rows = own.shape
    nblocks = len(blocks)
    tile = rows
    chunk = 512
    piece = 256
    held = nblocks * rows + chunk
    whole = lambda array: pl.BlockSpec(array.shape, lambda h, q: (0,) * array.ndim)
    sizes = (1, 8, HD)
    state_specs = [pl.BlockSpec((1, size, rows), lambda h, q: (h, 0, 0)) for size in sizes]
    first = state is None
    operands = [counts, pairw, own, *([] if first else blocks)]
    smem = pl.BlockSpec(memory_space=pltpu.SMEM)
    in_specs = [smem, smem, whole(own)] + [whole(block) for block in operands[3:]]
    if not first:
        operands += list(state)
        in_specs += state_specs
    if last:
        out_shape = jax.ShapeDtypeStruct((heads * HD, rows), jnp.bfloat16)
        out_specs = pl.BlockSpec((HD, rows), lambda h, q: (h, 0))
    else:
        out_shape = [jax.ShapeDtypeStruct((heads, size, rows), jnp.float32) for size in sizes]
        out_specs = state_specs
    pairs = heads * rows * nblocks * rows
    return pl.pallas_call(
        functools.partial(attention_kernel, nblocks, chunk, tile, piece, first, last),
        grid=(heads, rows // tile),
        in_specs=in_specs,
        out_specs=out_specs,
        out_shape=out_shape,
        scratch_shapes=[
            pltpu.VMEM((DEPTH, rows), jnp.float32),
            pltpu.VMEM((held, DEPTH), jnp.bfloat16),
            pltpu.VMEM((held, 128), jnp.float32),
            pltpu.VMEM((HD, held), jnp.bfloat16),
            pltpu.VMEM((DEPTH, rows), jnp.bfloat16),
            pltpu.VMEM((DEPTH, rows), jnp.bfloat16),
            pltpu.VMEM((DEPTH, rows), jnp.bfloat16),
            pltpu.VMEM((8, rows), jnp.float32),
        ],
        compiler_params=pltpu.CompilerParams(vmem_limit_bytes=48 * 1024 * 1024),
        cost_estimate=pl.CostEstimate(
            flops=pairs * 2 * DEPTH * 4, bytes_accessed=1 << 20, transcendentals=4 * pairs
        ),
        name="attend_last" if last else "attend_own",
    )(*operands)


def shards(hit_features, depth_kernel, point_weight, pair_weight, hit_order, valid_counts):
    rows = hit_features.shape[1]
    heads_here = point_weight.shape[0] // PROJ
    position = jnp.arange(rows, dtype=jnp.int32)
    chosen = (position[:, None] == hit_order[None, :]).astype(jnp.bfloat16)
    ordered = jnp.dot(hit_features, chosen, preferred_element_type=jnp.float32)
    ordered = ordered.astype(jnp.bfloat16)
    half = KSIZE // 2
    padded = with_halo(ordered, "seq", half).astype(jnp.float32)
    taps = depth_kernel.astype(jnp.float32)
    summed = jnp.zeros((ordered.shape[0], rows), jnp.float32)
    for offset in range(KSIZE):
        summed = summed + taps[offset][:, None] * padded[:, offset : offset + rows]
    smoothed = summed.astype(jnp.bfloat16)
    projected = jnp.dot(
        point_weight,
        lax.all_gather(smoothed, "head", axis=0, tiled=True),
        preferred_element_type=jnp.float32,
    )
    stored = projected.reshape(heads_here, PROJ, rows).astype(jnp.bfloat16)
    distances = (1, -1, -2)
    counts = jnp.concatenate([passed_along(valid_counts, "seq", d) for d in distances])
    mine = [stored[h : h + 1] for h in range(heads_here)]
    weights = [pair_weight[h : h + 1] for h in range(heads_here)]
    arrived = [[passed_along(one[:, HD:], "seq", d) for d in distances] for one in mine]
    states = [attend(valid_counts, w, one, [one], None, False) for w, one in zip(weights, mine)]
    results = [
        attend(counts, w, one, blocks, state, True)
        for w, one, blocks, state in zip(weights, mine, arrived, states)
    ]
    return jnp.concatenate(results, axis=0)


def solution(mesh):
    in_specs = (
        P("head", ("groups", "seq")),
        P(None, "head"),
        P("head", None),
        P("head", None),
        P(("groups", "seq")),
        P(("groups", "seq")),
    )
    out_specs = P("head", ("groups", "seq"))
    return jax.shard_map(shards, mesh=mesh, in_specs=in_specs, out_specs=out_specs, check_vma=False)
```
